256 devices in a mesh: rep: 16 (over x_hi, z), head: 8 (over y, core), pair: 2 (over x_lo).
Axes of the slice: x: 4 (x_hi: 2, x_lo: 2; x = x_hi * 2 + x_lo), y: 4, z: 8, core: 2. Of those that a mesh axis runs over, the one named last changes fastest.
Arguments:
- queries: bfloat16 [384, 8192], P(('rep', 'pair'), 'head'), may hold values from -24 to 24
- new_keys: bfloat16 [384, 1024], P(('rep', 'pair'), 'head'), may hold values from -6 to 6
- new_values: bfloat16 [384, 1024], P(('rep', 'pair'), 'head'), may hold values from -6 to 6
- key_cache: bfloat16 [384, 1024, 1024], P(('rep', 'pair'), None, 'head'), may hold values from -6 to 6
- value_cache: bfloat16 [384, 1024, 1024], P(('rep', 'pair'), None, 'head'), may hold values from -6 to 6
- lengths: int32 [384], P(('rep', 'pair')), may hold values from 2 to 1024
- residual: bfloat16 [384, 8192], P('head', ('rep', 'pair')), may hold values from -36 to 36
- norm_gain: float32 [8192], replicated, may hold values from 0.5 to 1.5
- out_weight: bfloat16 [8192, 8192], P('head', ('rep', 'pair')), may hold values from -0.5 to 0.5
- gate_weight: bfloat16 [8192, 28672], P('head', ('rep', 'pair')), may hold values from -0.0625 to 0.0625
- up_weight: bfloat16 [8192, 28672], P('head', ('rep', 'pair')), may hold values from -0.0625 to 0.0625
- down_weight: bfloat16 [28672, 8192], P(('rep', 'pair'), 'head'), may hold values from -0.03125 to 0.03125
Outputs:
- hidden_state: bfloat16 [384, 8192], P('head', ('rep', 'pair'))
- ffn_out: bfloat16 [384, 8192], P(('rep', 'pair'), 'head')
The draws below stay inside these ranges and needn't reach their ends.
Inputs may be any that keep to these rules, and one draw needn't show every extreme that they name: Cache slots 0 to lengths - 1 of a row are live, the others are ignored.
All inputs are finite; a program needn't handle non-finite values.
Results may differ from the reference program's by a relative error of at most 0.0095.
Values may be sent and summed in bfloat16 or wider, within the bound.
No kernel may reach another device: no remote copies, remote signals or barrier semaphores. Data moves between devices by JAX's collectives and lax.ppermute only.
A program may use at most 64 MiB of HBM per device.

```python
import jax
import jax.numpy as jnp
from jax import lax

D = 8192
FF = 28672
HEADS = 64
KV_HEADS = 8
HEAD_DIM = 128
CACHE = 1024
ROWS = 384
Q_WIDTH = 8192
KV_WIDTH = 1024


def drawn_cache_keys(key):
    base_key = jax.random.fold_in(key, 11)
    drawn_keys = jnp.clip(jax.random.normal(base_key, (ROWS, CACHE, KV_WIDTH), jnp.float32), -6.0, 6.0)
    return drawn_keys


def draw_key_cache(key, part):
    return drawn_cache_keys(key).astype(jnp.bfloat16)


def draw_queries(key, part):
    noise_key = jax.random.fold_in(key, 13)
    drawn = jnp.clip(jax.random.normal(noise_key, (ROWS, Q_WIDTH), jnp.float32), -6.0, 6.0)
    return drawn.astype(jnp.bfloat16)


def draw_residual(key, part):
    base_key = jax.random.fold_in(key, 17)
    drawn = jnp.clip(jax.random.normal(base_key, (ROWS, D), jnp.float32), -6.0, 6.0)
    return drawn.astype(jnp.bfloat16)


def place_ends(entries, stream_key, low, high):
    extent = entries.shape
    place = [jax.random.randint(jax.random.fold_in(stream_key, axis), (), 0, extent[axis]) for axis in range(len(extent))]
    entries = entries.at[tuple(place)].set(low)
    longest = extent.index(max(extent))
    place[longest] = (place[longest] + 1) % extent[longest]
    return entries.at[tuple(place)].set(high)


def block_scale(key, shape, shards, low, high):
    def one(dim, shards_of):
        draws = jax.random.uniform(jax.random.fold_in(jax.random.fold_in(key, 6), dim), (shards_of,), jnp.float32, low / len(shards), high / len(shards))
        return jnp.repeat(jnp.exp(draws), shape[dim] // shards_of).reshape((-1,) + (1,) * (len(shape) - dim - 1))

    level = one(*shards[0])
    for cut in shards[1:]:
        level = level * one(*cut)
    return level


def gaussian(key, dims, spread, reach, cuts=(), kind=jnp.bfloat16):
    entries = spread * jax.random.normal(key, dims, jnp.float32)
    if cuts:
        entries = entries * block_scale(key, dims, cuts, -0.22, 0.18)
    return jnp.clip(entries, -reach, reach).astype(kind)


def setup_inputs(seed: int = 0) -> dict:
    key_of = jax.random.split(jax.random.key(seed), 13)
    queries = draw_queries(jax.random.fold_in(key_of[12], 71), 0)
    new_keys = gaussian(key_of[1], (ROWS, KV_WIDTH), 1.0, 6.0, ((0, 32), (1, 8)))
    new_values = gaussian(key_of[2], (ROWS, KV_WIDTH), 1.0, 6.0, ((0, 32), (1, 8)))
    key_cache = draw_key_cache(jax.random.fold_in(key_of[12], 71), 0)
    value_cache = gaussian(key_of[4], (ROWS, CACHE, KV_WIDTH), 1.0, 6.0, ((0, 32), (2, 8)))
    lengths = place_ends(jax.random.randint(key_of[5], (ROWS,), 2, CACHE + 1), jax.random.fold_in(key_of[5], 1), 2, CACHE).astype(jnp.int32)
    residual = draw_residual(jax.random.fold_in(key_of[12], 71), 0)
    norm_gain = jnp.clip(1.0 + 0.1 * jax.random.normal(key_of[7], (D,), jnp.float32), 0.5, 1.5)
    out_weight = gaussian(key_of[8], (Q_WIDTH, D), (Q_WIDTH // 64) ** -0.5, 0.5, ((0, 8), (1, 32)))
    gate_weight = gaussian(key_of[9], (D, FF), D ** -0.5, 0.0625, ((0, 8), (1, 32)))
    up_weight = gaussian(key_of[10], (D, FF), D ** -0.5, 0.0625, ((0, 8), (1, 32)))
    down_weight = gaussian(key_of[11], (FF, D), FF ** -0.5, 0.03125, ((0, 32), (1, 8)))
    return {"queries": queries, "new_keys": new_keys, "new_values": new_values, "key_cache": key_cache, "value_cache": value_cache, "lengths": lengths, "residual": residual, "norm_gain": norm_gain, "out_weight": out_weight, "gate_weight": gate_weight, "up_weight": up_weight, "down_weight": down_weight}


def attend_row(row_item):
    query_row, key_new, value_new, cached_keys, cached_values, length = row_item
    group_size = HEADS // KV_HEADS
    score_scale = HEAD_DIM ** (-0.5)
    query_row = query_row.astype(jnp.float32).reshape(KV_HEADS, group_size, HEAD_DIM)
    cached_keys = cached_keys.astype(jnp.float32).reshape(CACHE, KV_HEADS, HEAD_DIM)
    cached_values = cached_values.astype(jnp.float32).reshape(CACHE, KV_HEADS, HEAD_DIM)
    key_new = key_new.astype(jnp.float32).reshape(KV_HEADS, HEAD_DIM)
    value_new = value_new.astype(jnp.float32).reshape(KV_HEADS, HEAD_DIM)
    scores = jnp.einsum('hgd,chd->hgc', query_row, cached_keys) * score_scale
    live_mask = jnp.arange(CACHE, dtype=jnp.int32) < length
    scores = jnp.where(live_mask[None, None, :], scores, -jnp.inf)
    own_score = jnp.einsum('hgd,hd->hg', query_row, key_new) * score_scale
    row_top = jnp.maximum(lax.optimization_barrier(jnp.max(scores, axis=2)), own_score)
    weights = jnp.exp(scores - row_top[:, :, None])
    own_weight = jnp.exp(own_score - row_top)
    weight_total = lax.optimization_barrier(jnp.sum(weights, axis=2)) + own_weight
    weights = lax.optimization_barrier(weights.astype(jnp.bfloat16)).astype(jnp.float32)
    own_weight = lax.optimization_barrier(own_weight.astype(jnp.bfloat16)).astype(jnp.float32)
    mixture = jnp.einsum('hgc,chd->hgd', weights, cached_values) + own_weight[:, :, None] * value_new[:, None, :]
    return (mixture / weight_total[:, :, None]).astype(jnp.bfloat16).reshape(HEADS * HEAD_DIM)

def reference(queries, new_keys, new_values, key_cache, value_cache, lengths, residual, norm_gain, out_weight, gate_weight, up_weight, down_weight):
    attn = lax.map(attend_row, (queries, new_keys, new_values, key_cache, value_cache, lengths))
    projected = jnp.dot(attn, out_weight, preferred_element_type=jnp.float32)
    hidden_state = (residual.astype(jnp.float32) + projected).astype(jnp.bfloat16)
    state_f = hidden_state.astype(jnp.float32)
    mean_square = lax.optimization_barrier(jnp.mean(state_f * state_f, axis=1, keepdims=True))
    normed = (state_f * lax.rsqrt(mean_square + 1e-05) * norm_gain).astype(jnp.bfloat16)
    gate_full = jnp.dot(normed, gate_weight, preferred_element_type=jnp.float32)
    up_full = jnp.dot(normed, up_weight, preferred_element_type=jnp.float32)
    hidden = (jax.nn.silu(gate_full) * up_full).astype(jnp.bfloat16)
    ffn_out = jnp.dot(hidden, down_weight, preferred_element_type=jnp.float32).astype(jnp.bfloat16)
    return (hidden_state, ffn_out)
```

```python
import jax
import jax.numpy as jnp
from jax import lax
from jax.sharding import Mesh, PartitionSpec as P

HEADS = 64
KV_HEADS = 8
HEAD_DIM = 128
D = 8192
X = ("xh", "xl")
HEAD = ("y", "c")
ALL = ("xh", "z", "y", "c", "xl")
BF = jnp.bfloat16
F4 = jnp.float32


def shift(array, axis, size, step):
    return lax.ppermute(array, axis, [(i, (i + step) % size) for i in range(size)])


def copies_by_a2a(array, axis, size):
    copies = jnp.broadcast_to(array, (size, *array.shape))
    return lax.all_to_all(copies, axis, 0, 0, tiled=True)


def gather4(array, axis, me):
    got = [array] + [shift(array, axis, 4, k) for k in (1, 3, 2)]
    rel = jnp.stack([got[0], got[1], got[3], got[2]])
    return jnp.stack([lax.dynamic_index_in_dim(rel, (me - j) % 4, 0, False) for j in range(4)])


def summed4(pieces, axis, me):
    send = lambda k: lax.dynamic_index_in_dim(pieces, (me + k) % 4, 0, False).astype(BF)
    got = [shift(send(k), axis, 4, k) for k in (1, 3, 2)]
    own = lax.dynamic_index_in_dim(pieces, me, 0, False).astype(F4)
    return own + got[0].astype(F4) + got[1].astype(F4) + got[2].astype(F4)


def swapped(array, axis):
    return lax.ppermute(array, axis, [(0, 1), (1, 0)])


def transpose_perm():
    pairs = []
    for xh in range(2):
        for z in range(8):
            for y in range(4):
                for c in range(2):
                    for xl in range(2):
                        src = (((xh * 8 + z) * 4 + y) * 2 + c) * 2 + xl
                        z2, z1, z0 = z >> 2, (z >> 1) & 1, z & 1
                        nxh, nz = y >> 1, ((y & 1) << 2) | (c << 1) | z0
                        ny, nc = xh * 2 + z2, z1
                        pairs.append((src, (((nxh * 8 + nz) * 4 + ny) * 2 + nc) * 2 + xl))
    return pairs


def attention(queries, new_keys, new_values, key_cache, value_cache, lengths):
    row_count = queries.shape[0]
    slot_count = key_cache.shape[1]
    group_size = HEADS // KV_HEADS
    scale = HEAD_DIM ** (-0.5)
    q = queries.reshape(row_count, group_size, HEAD_DIM)
    scores = jnp.einsum("rgd,rcd->rgc", q, key_cache, preferred_element_type=F4) * scale
    slot_ids = lax.broadcasted_iota(jnp.int32, (row_count, 1, slot_count), 2)
    scores = jnp.where(slot_ids < lengths[:, None, None], scores, -jnp.inf)
    own_score = jnp.einsum("rgd,rd->rg", q, new_keys, preferred_element_type=F4) * scale
    top = jnp.maximum(jnp.max(scores, axis=2), own_score)
    weights = jnp.exp(scores - top[..., None])
    own_weight = jnp.exp(own_score - top)
    total = jnp.sum(weights, axis=2) + own_weight
    own_low = own_weight.astype(BF).astype(F4)
    mixture = jnp.einsum("rgc,rcd->rgd", weights.astype(BF), value_cache, preferred_element_type=F4)
    mixture = mixture + own_low[..., None] * new_values.astype(F4)[:, None, :]
    return (mixture / total[..., None]).astype(BF).reshape(row_count, -1)


def local(
    queries,
    new_keys,
    new_values,
    key_cache,
    value_cache,
    lengths,
    residual,
    norm_gain,
    out_weight,
    gate_weight,
    up_weight,
    down_weight,
):
    x = lax.axis_index("xh") * 2 + lax.axis_index("xl")
    y = lax.axis_index("y")
    c = lax.axis_index("c")
    head = y * 2 + c
    res = residual.reshape(2, 2, 12, 256).swapaxes(0, 1).reshape(48, 256).astype(F4)
    gain = lax.dynamic_slice_in_dim(norm_gain, head * 1024, 1024, 0)

    attn = attention(queries, new_keys, new_values, key_cache, value_cache, lengths)
    along_z = copies_by_a2a(attn, "z", 8).reshape(96, 1024)
    rows = gather4(along_z, X, x)
    projected = jnp.dot(rows.reshape(384, 1024), out_weight, preferred_element_type=F4)
    pieces = projected.astype(BF).reshape(2, 2, 4, 24, 256).swapaxes(1, 2).reshape(8, 48, 256)
    pieces = lax.all_to_all(pieces, HEAD, 0, 0, tiled=True)
    state = (res + jnp.sum(pieces.astype(F4), axis=0)).astype(BF)
    hidden_state = state.reshape(2, 2, 12, 256).swapaxes(0, 1).reshape(48, 256)

    moved = lax.ppermute(state, ALL, transpose_perm())
    along_z = copies_by_a2a(moved, "z", 8)
    along_z = along_z.reshape(4, 2, 48, 256).swapaxes(1, 2).reshape(192, 512)
    full = gather4(along_z, X, x).reshape(2, 2, 192, 2, 256)
    full = full.transpose(0, 2, 3, 1, 4).reshape(384, 1024)
    full_f = full.astype(F4)
    squares = jnp.sum(full_f * full_f, axis=1, keepdims=True)
    scaled = (full_f * gain).astype(BF)
    gate = jnp.dot(scaled, gate_weight, preferred_element_type=F4)
    up = jnp.dot(scaled, up_weight, preferred_element_type=F4)
    sq_hi = squares.astype(BF)
    sq_lo = (squares - sq_hi.astype(F4)).astype(BF)
    lanes = lax.broadcasted_iota(jnp.int32, (1, 128), 1)
    sq = jnp.where(lanes == 0, sq_hi.astype(F4), jnp.where(lanes == 1, sq_lo.astype(F4), 0.0))
    both = jnp.concatenate([gate, up, sq], axis=1)
    both = both.reshape(4, 2, 48, 1920)
    other = lax.dynamic_index_in_dim(both, 1 - c, 1, False).astype(BF)
    mine = lax.dynamic_index_in_dim(both, c, 1, False)
    pair_sum = mine + swapped(other, "c").astype(F4)
    share = summed4(pair_sum, "y", y)
    mean_square = jnp.sum(share[:, 1792:], axis=1, keepdims=True) / D
    inv = lax.rsqrt(mean_square + 1e-05)
    gate = share[:, :896] * inv
    up = share[:, 896:1792] * inv
    hidden = (jax.nn.silu(gate) * up).astype(BF)
    hidden = gather4(hidden, "y", y)
    theirs = swapped(hidden, "c")
    both = jnp.stack([jnp.where(c == 0, hidden, theirs), jnp.where(c == 0, theirs, hidden)], axis=1)
    hidden = both.reshape(384, 896)

    part = jnp.dot(hidden, down_weight, preferred_element_type=F4)
    part = part.reshape(2, 4, 2, 24, 1024).swapaxes(1, 2).reshape(4, 96, 1024)
    part = summed4(part, X, x).astype(BF).reshape(8, 12, 1024)
    part = lax.all_to_all(part, "z", 0, 0, tiled=True)
    ffn_out = jnp.sum(part.astype(F4), axis=0).astype(BF)
    return (hidden_state, ffn_out)


def solution(mesh):
    fine = Mesh(mesh.devices.reshape(2, 8, 4, 2, 2), ALL)
    plane = ("xh", "z", "xl")
    placed = (
        P(plane, HEAD),
        P(plane, HEAD),
        P(plane, HEAD),
        P(plane, None, HEAD),
        P(plane, None, HEAD),
        P(plane),
        P(HEAD, plane),
        P(),
        P(HEAD, plane),
        P(HEAD, plane),
        P(HEAD, plane),
        P(plane, HEAD),
    )
    return jax.shard_map(
        local,
        mesh=fine,
        in_specs=placed,
        out_specs=(P(HEAD, plane), P(plane, HEAD)),
        check_vma=False,
    )
```

```python
import jax
import jax.numpy as jnp
from jax import lax
from jax.experimental import pallas as pl
from jax.experimental.pallas import tpu as pltpu
from jax.sharding import Mesh, PartitionSpec as P

HEADS = 64
KV_HEADS = 8
HEAD_DIM = 128
D = 8192
X = ("xh", "xl")
HEAD = ("y", "c")
ALL = ("xh", "z", "y", "c", "xl")
BF = jnp.bfloat16
F4 = jnp.float32


def shift(array, axis, size, step):
    return lax.ppermute(array, axis, [(i, (i + step) % size) for i in range(size)])


def copies_by_a2a(array, axis, size):
    copies = jnp.broadcast_to(array, (size, *array.shape))
    return lax.all_to_all(copies, axis, 0, 0, tiled=True)


def gather4(array, axis, me):
    got = [array] + [shift(array, axis, 4, k) for k in (1, 3, 2)]
    rel = jnp.stack([got[0], got[1], got[3], got[2]])
    return jnp.stack([lax.dynamic_index_in_dim(rel, (me - j) % 4, 0, False) for j in range(4)])


def summed4(pieces, axis, me):
    send = lambda k: lax.dynamic_index_in_dim(pieces, (me + k) % 4, 0, False).astype(BF)
    got = [shift(send(k), axis, 4, k) for k in (1, 3, 2)]
    own = lax.dynamic_index_in_dim(pieces, me, 0, False).astype(F4)
    return own + got[0].astype(F4) + got[1].astype(F4) + got[2].astype(F4)


def swapped(array, axis):
    return lax.ppermute(array, axis, [(0, 1), (1, 0)])


def transpose_perm():
    pairs = []
    for xh in range(2):
        for z in range(8):
            for y in range(4):
                for c in range(2):
                    for xl in range(2):
                        src = (((xh * 8 + z) * 4 + y) * 2 + c) * 2 + xl
                        z2, z1, z0 = z >> 2, (z >> 1) & 1, z & 1
                        nxh, nz = y >> 1, ((y & 1) << 2) | (c << 1) | z0
                        ny, nc = xh * 2 + z2, z1
                        pairs.append((src, (((nxh * 8 + nz) * 4 + ny) * 2 + nc) * 2 + xl))
    return pairs


def attention(queries, new_keys, new_values, key_cache, value_cache, lengths):
    row_count = queries.shape[0]
    slot_count = key_cache.shape[1]
    group_size = HEADS // KV_HEADS
    scale = HEAD_DIM ** (-0.5)
    q = queries.reshape(row_count, group_size, HEAD_DIM)
    scores = jnp.einsum("rgd,rcd->rgc", q, key_cache, preferred_element_type=F4) * scale
    slot_ids = lax.broadcasted_iota(jnp.int32, (row_count, 1, slot_count), 2)
    scores = jnp.where(slot_ids < lengths[:, None, None], scores, -jnp.inf)
    own_score = jnp.einsum("rgd,rd->rg", q, new_keys, preferred_element_type=F4) * scale
    top = jnp.maximum(jnp.max(scores, axis=2), own_score)
    weights = jnp.exp(scores - top[..., None])
    own_weight = jnp.exp(own_score - top)
    total = jnp.sum(weights, axis=2) + own_weight
    own_low = own_weight.astype(BF).astype(F4)
    mixture = jnp.einsum("rgc,rcd->rgd", weights.astype(BF), value_cache, preferred_element_type=F4)
    mixture = mixture + own_low[..., None] * new_values.astype(F4)[:, None, :]
    return (mixture / total[..., None]).astype(BF).reshape(row_count, -1)


VM = pl.BlockSpec(memory_space=pltpu.VMEM)
SM = pl.BlockSpec(memory_space=pltpu.SMEM)
N_CUTS = ((0, 256), (256, 256), (512, 256), (768, 128))


def call(body, outs, ins, scratch=(), flops=0):
    moved = sum(a.size * a.dtype.itemsize for a in ins)
    return pl.pallas_call(
        body,
        out_shape=outs,
        in_specs=[SM] + [VM] * (len(ins) - 1),
        out_specs=jax.tree.map(lambda _: VM, outs),
        scratch_shapes=list(scratch),
        compiler_params=pltpu.CompilerParams(vmem_limit_bytes=40 * 1024 * 1024),
        cost_estimate=pl.CostEstimate(flops=flops, bytes_accessed=moved, transcendentals=0),
    )(*ins)


def sds(shape, dtype):
    return jax.ShapeDtypeStruct(shape, dtype)


def proj_body(at, p0, p1, p2, p3, w, out):
    for k, p in enumerate((p0, p1, p2, p3)):
        src = lax.rem(at[0] + 4 - k, 4)
        xh, xl = lax.div(src, 2), lax.rem(src, 2)
        part = jnp.dot(p[...], w[...], preferred_element_type=F4)
        for j in range(4):
            out[xh * 4 + j, xl] = part[24 * j : 24 * j + 24].astype(BF)


def proj(at, pieces, weight):
    out = call(proj_body, sds((8, 2, 24, 256), BF), [at, *pieces, weight], flops=2 * 384 * 1024 * 256)
    return out.reshape(8, 48, 256)


def up_body(half, at, p0, p1, p2, p3, gain, wg, wu, out, rows, squares):
    z1 = at[2] if half == 0 else 1 - at[2]
    squares[...] = jnp.zeros_like(squares)
    for k, p in enumerate((p0, p1, p2, p3)):
        src = lax.rem(at[0] + 4 - k, 4)
        xh, xl = lax.div(src, 2), lax.rem(src, 2)
        for z2 in range(2):
            for z0 in range(2):
                part = p[z2 * 4 + z1 * 2 + z0].astype(F4)
                col = pl.multiple_of(z0 * 512 + xl * 256, 256)
                row = pl.multiple_of(xh * 96 + z2 * 48, 48)
                sq = part * part
                squares[pl.ds(row, 48), :] += sq[:, :128] + sq[:, 128:]
                rows[pl.ds(row, 48), pl.ds(col, 256)] = (part * gain[:, pl.ds(col, 256)]).astype(BF)
    total = jnp.sum(squares[...], axis=1, keepdims=True)
    high = total.astype(BF).astype(F4)
    lanes = lax.broadcasted_iota(jnp.int32, (192, 128), 1)
    tail = jnp.where(lanes == 0, high, jnp.where(lanes == 1, total - high, 0.0))
    left = rows[...]
    for base, w in ((0, wg), (896, wu)):
        for at_col, size in N_CUTS:
            part = jnp.dot(left, w[:, at_col : at_col + size], preferred_element_type=F4)
            part = part.astype(out.dtype).reshape(4, 48, size)
            out[:, :, base + at_col : base + at_col + size] = part
    out[:, :, 1792:] = tail.astype(out.dtype).reshape(4, 48, 128)


def up_half(half, dtype, at, pieces, gain, wg, wu):
    return call(
        lambda *refs: up_body(half, *refs),
        sds((4, 48, 1920), dtype),
        [at, *pieces, gain, wg, wu],
        [pltpu.VMEM((192, 1024), BF), pltpu.VMEM((192, 128), F4)],
        flops=2 * 192 * 1024 * 1792,
    )


def pair_body(at, mine, theirs, own, s1, s2, s3):
    y = at[1]
    own[...] = mine[y] + theirs[y].astype(F4)
    for k, ref in ((1, s1), (2, s2), (3, s3)):
        to = lax.rem(y + k, 4)
        ref[...] = (mine[to] + theirs[to].astype(F4)).astype(BF)


def pair_sums(at, mine, theirs):
    outs = [sds((48, 1920), F4)] + [sds((48, 1920), BF)] * 3
    return call(pair_body, outs, [at, mine, theirs])


def hidden_body(at, own, r1, r2, r3, out):
    add = lambda lo, hi: (
        own[:, lo:hi] + r1[:, lo:hi].astype(F4) + r2[:, lo:hi].astype(F4) + r3[:, lo:hi].astype(F4)
    )
    mean_square = jnp.sum(add(1792, 1920), axis=1, keepdims=True) / D
    inv = lax.rsqrt(mean_square + 1e-05)
    gate = add(0, 896) * inv
    up = add(896, 1792) * inv
    out[...] = (gate / (1.0 + jnp.exp(-gate)) * up).astype(BF)


def order_body(at, p0, p1, p2, p3, out):
    for k, p in enumerate((p0, p1, p2, p3)):
        out[lax.rem(at[1] + 4 - k, 4)] = p[...]


def down_body(at, mine, theirs, w, own, s1, s2, s3, acc):
    for rows, z1 in ((mine, at[2]), (theirs, 1 - at[2])):
        left = rows[...].reshape(192, 896)
        for n in range(4):
            part = jnp.dot(left, w[:, 256 * n : 256 * n + 256], preferred_element_type=F4)
            for b in range(4):
                for xl in range(2):
                    r = b * 48 + xl * 24
                    acc[(b // 2) * 2 + xl, (b % 2) * 2 + z1, :, 256 * n : 256 * n + 256] = part[r : r + 24]
    own[...] = acc[at[0]]
    for k, ref in ((1, s1), (2, s2), (3, s3)):
        ref[...] = acc[lax.rem(at[0] + k, 4)].astype(BF)


def down(at, mine, theirs, weight):
    outs = [sds((4, 24, 1024), F4)] + [sds((4, 24, 1024), BF)] * 3
    return call(
        down_body,
        outs,
        [at, mine, theirs, weight],
        [pltpu.VMEM((4, 4, 24, 1024), F4)],
        flops=2 * 384 * 896 * 1024,
    )


def around(array, axis):
    got = {k: shift(array, axis, 4, k) for k in (2, 1, 3)}
    return [got[1], got[2], got[3]]


def sent(one, two, three, axis):
    got = {k: shift(a, axis, 4, k) for k, a in ((2, two), (1, one), (3, three))}
    return [got[1], got[2], got[3]]


def local(
    queries,
    new_keys,
    new_values,
    key_cache,
    value_cache,
    lengths,
    residual,
    norm_gain,
    out_weight,
    gate_weight,
    up_weight,
    down_weight,
):
    x = lax.axis_index("xh") * 2 + lax.axis_index("xl")
    y = lax.axis_index("y")
    c = lax.axis_index("c")
    at = jnp.stack([x, y, c, c]).astype(jnp.int32)
    res = residual.reshape(2, 2, 12, 256).swapaxes(0, 1).reshape(48, 256).astype(F4)
    gain = lax.dynamic_slice_in_dim(norm_gain, (y * 2 + c) * 1024, 1024, 0).reshape(1, 1024)

    attn = attention(queries, new_keys, new_values, key_cache, value_cache, lengths)
    along_z = copies_by_a2a(attn, "z", 8).reshape(96, 1024)
    pieces = proj(at, [along_z, *around(along_z, X)], out_weight)
    pieces = lax.all_to_all(pieces, HEAD, 0, 0, tiled=True)
    state = (res + jnp.sum(pieces.astype(F4), axis=0)).astype(BF)
    hidden_state = state.reshape(2, 2, 12, 256).swapaxes(0, 1).reshape(48, 256)

    moved = lax.ppermute(state, ALL, transpose_perm())
    along_z = copies_by_a2a(moved, "z", 8)
    pieces = [along_z, *around(along_z, X)]
    other = up_half(1, BF, at, pieces, gain, gate_weight, up_weight)
    theirs = swapped(other, "c")
    mine = up_half(0, F4, at, pieces, gain, gate_weight, up_weight)
    own, *shares = pair_sums(at, mine, theirs)
    hidden = call(hidden_body, sds((48, 896), BF), [at, own, *sent(*shares, "y")])
    hidden = call(order_body, sds((4, 48, 896), BF), [at, hidden, *around(hidden, "y")])
    own, *shares = down(at, hidden, swapped(hidden, "c"), down_weight)
    part = own
    for got in sent(*shares, X):
        part = part + got.astype(F4)
    part = part.astype(BF).reshape(8, 12, 1024)
    part = lax.all_to_all(part, "z", 0, 0, tiled=True)
    ffn_out = jnp.sum(part.astype(F4), axis=0).astype(BF)
    return (hidden_state, ffn_out)


def solution(mesh):
    fine = Mesh(mesh.devices.reshape(2, 8, 4, 2, 2), ALL)
    plane = ("xh", "z", "xl")
    placed = (
        P(plane, HEAD),
        P(plane, HEAD),
        P(plane, HEAD),
        P(plane, None, HEAD),
        P(plane, None, HEAD),
        P(plane),
        P(HEAD, plane),
        P(),
        P(HEAD, plane),
        P(HEAD, plane),
        P(HEAD, plane),
        P(plane, HEAD),
    )
    return jax.shard_map(
        local,
        mesh=fine,
        in_specs=placed,
        out_specs=(P(HEAD, plane), P(plane, HEAD)),
        check_vma=False,
    )
```

```python
import jax
import jax.numpy as jnp
from jax import lax
from jax.experimental import pallas as pl
from jax.experimental.pallas import tpu as pltpu
from jax.sharding import Mesh, PartitionSpec as P

HEADS = 64
KV_HEADS = 8
HEAD_DIM = 128
D = 8192
X = ("xh", "xl")
HEAD = ("y", "c")
ALL = ("xh", "z", "y", "c", "xl")
BF = jnp.bfloat16
F4 = jnp.float32


def shift(array, axis, size, step):
    return lax.ppermute(array, axis, [(i, (i + step) % size) for i in range(size)])


def copies_by_a2a(array, axis, size):
    copies = jnp.broadcast_to(array, (size, *array.shape))
    return lax.all_to_all(copies, axis, 0, 0, tiled=True)


def gather4(array, axis, me):
    got = [array] + [shift(array, axis, 4, k) for k in (1, 3, 2)]
    rel = jnp.stack([got[0], got[1], got[3], got[2]])
    return jnp.stack([lax.dynamic_index_in_dim(rel, (me - j) % 4, 0, False) for j in range(4)])


def summed4(pieces, axis, me):
    send = lambda k: lax.dynamic_index_in_dim(pieces, (me + k) % 4, 0, False).astype(BF)
    got = [shift(send(k), axis, 4, k) for k in (1, 3, 2)]
    own = lax.dynamic_index_in_dim(pieces, me, 0, False).astype(F4)
    return own + got[0].astype(F4) + got[1].astype(F4) + got[2].astype(F4)


def swapped(array, axis):
    return lax.ppermute(array, axis, [(0, 1), (1, 0)])


def device_pairs(place):
    pairs = []
    for xh in range(2):
        for z in range(8):
            for y in range(4):
                for c in range(2):
                    for xl in range(2):
                        src = (((xh * 8 + z) * 4 + y) * 2 + c) * 2 + xl
                        nxh, nz, ny, nc, nxl = place(xh, z, y, c, xl)
                        pairs.append((src, (((nxh * 8 + nz) * 4 + ny) * 2 + nc) * 2 + nxl))
    return pairs


def to_features(xh, z, y, c, xl):
    return xh, ((y & 1) << 2) | (c << 1) | (z & 1), (y & 2) | (z >> 2), (z >> 1) & 1, xl


def swap_same(xh, z, y, c, xl):
    return y >> 1, z, (xh << 1) | (y & 1), c, xl


def swap_cross(xh, z, y, c, xl):
    return y >> 1, z, (xh << 1) | (y & 1), c, 1 - xl


def attention(queries, new_keys, new_values, key_cache, value_cache, lengths):
    row_count = queries.shape[0]
    slot_count = key_cache.shape[1]
    group_size = HEADS // KV_HEADS
    scale = HEAD_DIM ** (-0.5)
    q = queries.reshape(row_count, group_size, HEAD_DIM)
    scores = jnp.einsum("rgd,rcd->rgc", q, key_cache, preferred_element_type=F4) * scale
    slot_ids = lax.broadcasted_iota(jnp.int32, (row_count, 1, slot_count), 2)
    scores = jnp.where(slot_ids < lengths[:, None, None], scores, -jnp.inf)
    own_score = jnp.einsum("rgd,rd->rg", q, new_keys, preferred_element_type=F4) * scale
    top = jnp.maximum(jnp.max(scores, axis=2), own_score)
    weights = jnp.exp(scores - top[..., None])
    own_weight = jnp.exp(own_score - top)
    total = jnp.sum(weights, axis=2) + own_weight
    own_low = own_weight.astype(BF).astype(F4)
    mixture = jnp.einsum("rgc,rcd->rgd", weights.astype(BF), value_cache, preferred_element_type=F4)
    mixture = mixture + own_low[..., None] * new_values.astype(F4)[:, None, :]
    return (mixture / total[..., None]).astype(BF).reshape(row_count, -1)


VM = pl.BlockSpec(memory_space=pltpu.VMEM)
SM = pl.BlockSpec(memory_space=pltpu.SMEM)
N_CUTS = ((0, 256), (256, 256), (512, 256), (768, 128))


def call(body, outs, ins, scratch=(), flops=0):
    moved = sum(a.size * a.dtype.itemsize for a in ins)
    return pl.pallas_call(
        body,
        out_shape=outs,
        in_specs=[SM] + [VM] * (len(ins) - 1),
        out_specs=jax.tree.map(lambda _: VM, outs),
        scratch_shapes=list(scratch),
        compiler_params=pltpu.CompilerParams(vmem_limit_bytes=40 * 1024 * 1024),
        cost_estimate=pl.CostEstimate(flops=flops, bytes_accessed=moved, transcendentals=0),
    )(*ins)


def sds(shape, dtype):
    return jax.ShapeDtypeStruct(shape, dtype)


def proj_body(at, rows, w0, w1, w2, w3, out, held, sems):
    copies = [pltpu.make_async_copy(w, held.at[k], sems.at[k]) for k, w in enumerate((w0, w1, w2, w3))]
    for copy in copies:
        copy.start()
    left = rows[...]
    for k, copy in enumerate(copies):
        src = lax.rem(at[0] + 4 - k, 4)
        xh, xl = lax.div(src, 2), lax.rem(src, 2)
        copy.wait()
        part = jnp.dot(left, held[k], preferred_element_type=F4)
        for j in range(4):
            out[xh * 4 + j, xl] = part[24 * j : 24 * j + 24].astype(BF)


def proj(at, rows, weights):
    moved = 4 * 1024 * 256 * 2
    return pl.pallas_call(
        proj_body,
        out_shape=sds((8, 2, 24, 256), BF),
        in_specs=[SM, VM] + [pl.BlockSpec(memory_space=pl.ANY)] * 4,
        out_specs=VM,
        scratch_shapes=[pltpu.VMEM((4, 1024, 256), BF), pltpu.SemaphoreType.DMA((4,))],
        cost_estimate=pl.CostEstimate(flops=2 * 96 * 1024 * 1024, bytes_accessed=moved, transcendentals=0),
    )(at, rows, *weights)


def first_body(at, p0, wg, wu, out):
    part = p0[...].astype(F4)
    part = part * part
    out[...] = part[:, :, :128] + part[:, :, 128:256] + part[:, :, 256:384] + part[:, :, 384:]


def up_body(half, at, sq0, p0, p1, p2, p3, gain, wg, wu, out, rows, squares):
    z1 = at[2] if half == 0 else 1 - at[2]
    for k, p in enumerate((p0, p1, p2, p3)):
        src = lax.rem(at[0] + 4 - k, 4)
        xh, xl = lax.div(src, 2), lax.rem(src, 2)
        for z2 in range(2):
            row = pl.multiple_of(xh * 96 + z2 * 48 + xl * 24, 8)
            sq = None
            for z0 in range(2):
                place = z2 * 4 + z1 * 2 + z0
                part = p[place].astype(F4)
                cols = slice(z0 * 512, z0 * 512 + 512)
                rows[pl.ds(row, 24), cols] = part * gain[:, cols]
                if k == 0:
                    one = sq0[place]
                else:
                    part = part * part
                    one = part[:, :128] + part[:, 128:256] + part[:, 256:384] + part[:, 384:]
                sq = one if sq is None else sq + one
            squares[pl.ds(row, 24), :] = sq
    total = jnp.sum(squares[...], axis=1, keepdims=True)
    high = total.astype(BF).astype(F4)
    lanes = lax.broadcasted_iota(jnp.int32, (192, 128), 1)
    tail = jnp.where(lanes == 0, high, jnp.where(lanes == 1, total - high, 0.0))
    left = rows[...].astype(BF)
    for base, w in ((0, wg), (896, wu)):
        for at_col, size in N_CUTS:
            part = jnp.dot(left, w[:, at_col : at_col + size], preferred_element_type=F4)
            part = part.astype(out.dtype).reshape(4, 48, size)
            out[:, :, base + at_col : base + at_col + size] = part
    out[:, :, 1792:] = tail.astype(out.dtype).reshape(4, 48, 128)


def up_half(half, dtype, at, sq0, pieces, gain, wg, wu):
    return call(
        lambda *refs: up_body(half, *refs),
        sds((4, 48, 1920), dtype),
        [at, sq0, *pieces, gain, wg, wu],
        [pltpu.VMEM((192, 1024), F4), pltpu.VMEM((192, 128), F4)],
        flops=2 * 192 * 1024 * 1792,
    )


def pair_body(at, mine, theirs, own, s1, s2, s3):
    y = at[1]
    own[...] = mine[y] + theirs[y].astype(F4)
    for k, ref in ((1, s1), (2, s2), (3, s3)):
        to = lax.rem(y + k, 4)
        ref[...] = (mine[to] + theirs[to].astype(F4)).astype(BF)


def pair_sums(at, mine, theirs):
    outs = [sds((48, 1920), F4)] + [sds((48, 1920), BF)] * 3
    return call(pair_body, outs, [at, mine, theirs])


def hidden_body(at, own, r1, r2, r3, out):
    add = lambda lo, hi: (
        own[:, lo:hi] + r1[:, lo:hi].astype(F4) + r2[:, lo:hi].astype(F4) + r3[:, lo:hi].astype(F4)
    )
    mean_square = jnp.sum(add(1792, 1920), axis=1, keepdims=True) / D
    inv = lax.rsqrt(mean_square + 1e-05)
    gate = add(0, 896) * inv
    up = add(896, 1792) * inv
    out[...] = (gate / (1.0 + jnp.exp(-gate)) * up).astype(BF)


def order_body(at, p0, p1, p2, p3, out):
    for k, p in enumerate((p0, p1, p2, p3)):
        out[lax.rem(at[1] + 4 - k, 4)] = p[...]


def down_body(at, mine, theirs, w, own, s1, s2, s3, acc):
    for rows, z1 in ((mine, at[2]), (theirs, 1 - at[2])):
        left = rows[...].reshape(192, 896)
        for n in range(4):
            part = jnp.dot(left, w[:, 256 * n : 256 * n + 256], preferred_element_type=F4)
            for b in range(4):
                for xl in range(2):
                    r = b * 48 + xl * 24
                    acc[(b // 2) * 2 + xl, (b % 2) * 2 + z1, :, 256 * n : 256 * n + 256] = part[r : r + 24]
    own[...] = acc[at[0]]
    for k, ref in ((1, s1), (2, s2), (3, s3)):
        ref[...] = acc[lax.rem(at[0] + k, 4)].astype(BF)


def down(at, mine, theirs, weight):
    outs = [sds((4, 24, 1024), F4)] + [sds((4, 24, 1024), BF)] * 3
    return call(
        down_body,
        outs,
        [at, mine, theirs, weight],
        [pltpu.VMEM((4, 4, 24, 1024), F4)],
        flops=2 * 384 * 896 * 1024,
    )


def around(array, axis):
    got = {k: shift(array, axis, 4, k) for k in (2, 1, 3)}
    return [got[1], got[2], got[3]]


def sent(one, two, three, axis):
    got = {k: shift(a, axis, 4, k) for k, a in ((2, two), (1, one), (3, three))}
    return [got[1], got[2], got[3]]


def local(
    queries,
    new_keys,
    new_values,
    key_cache,
    value_cache,
    lengths,
    residual,
    norm_gain,
    out_weight,
    gate_weight,
    up_weight,
    down_weight,
):
    x = lax.axis_index("xh") * 2 + lax.axis_index("xl")
    y = lax.axis_index("y")
    c = lax.axis_index("c")
    at = jnp.stack([x, y, c, c]).astype(jnp.int32)
    xl = lax.axis_index("xl")
    gain = lax.dynamic_slice_in_dim(norm_gain, (y * 2 + c) * 1024, 1024, 0).reshape(1, 1024)
    weights = [out_weight, *around(out_weight, X)]

    attn = attention(queries, new_keys, new_values, key_cache, value_cache, lengths)
    rows = copies_by_a2a(attn, "z", 8).reshape(96, 1024)
    res = residual.reshape(2, 2, 12, 256).swapaxes(0, 1)
    res, rows = lax.optimization_barrier((res, rows))
    res_same = lax.dynamic_index_in_dim(res, xl, 0, False).reshape(24, 256)
    res_cross = lax.dynamic_index_in_dim(res, 1 - xl, 0, False).reshape(24, 256)
    res_same = lax.ppermute(res_same, ALL, device_pairs(swap_same))
    res_cross = lax.ppermute(res_cross, ALL, device_pairs(swap_cross))
    first = jnp.where(xl == 0, res_same, res_cross).astype(F4)
    second = jnp.where(xl == 0, res_cross, res_same).astype(F4)
    pieces = lax.all_to_all(proj(at, rows, weights), HEAD, 0, 0, tiled=True)
    state = jnp.sum(pieces.astype(F4), axis=0) + jnp.stack([first, second])
    state = state.astype(BF)

    moved = state.swapaxes(0, 1).reshape(24, 512)
    moved = lax.ppermute(moved, ALL, device_pairs(to_features))
    out_same = lax.dynamic_index_in_dim(state, xl, 0, False)
    out_cross = lax.dynamic_index_in_dim(state, 1 - xl, 0, False)
    out_same = lax.ppermute(out_same, ALL, device_pairs(swap_same))
    out_cross = lax.ppermute(out_cross, ALL, device_pairs(swap_cross))
    hidden_state = jnp.stack([jnp.where(xl == 0, out_same, out_cross), jnp.where(xl == 0, out_cross, out_same)])
    hidden_state = hidden_state.reshape(2, 2, 12, 256).swapaxes(0, 1).reshape(48, 256)

    along_z = copies_by_a2a(moved, "z", 8)
    pieces = [along_z, *around(along_z, X)]
    sq0 = call(first_body, sds((8, 24, 128), F4), [at, along_z, gate_weight, up_weight])
    other = up_half(1, BF, at, sq0, pieces, gain, gate_weight, up_weight)
    theirs = swapped(other, "c")
    mine = up_half(0, F4, at, sq0, pieces, gain, gate_weight, up_weight)
    own, *shares = pair_sums(at, mine, theirs)
    hidden = call(hidden_body, sds((48, 896), BF), [at, own, *sent(*shares, "y")])
    hidden = call(order_body, sds((4, 48, 896), BF), [at, hidden, *around(hidden, "y")])
    own, *shares = down(at, hidden, swapped(hidden, "c"), down_weight)
    part = own
    for got in sent(*shares, X):
        part = part + got.astype(F4)
    part = part.astype(BF).reshape(8, 12, 1024)
    part = lax.all_to_all(part, "z", 0, 0, tiled=True)
    ffn_out = jnp.sum(part.astype(F4), axis=0).astype(BF)
    return (hidden_state, ffn_out)


def solution(mesh):
    fine = Mesh(mesh.devices.reshape(2, 8, 4, 2, 2), ALL)
    plane = ("xh", "z", "xl")
    placed = (
        P(plane, HEAD),
        P(plane, HEAD),
        P(plane, HEAD),
        P(plane, None, HEAD),
        P(plane, None, HEAD),
        P(plane),
        P(HEAD, plane),
        P(),
        P(HEAD, plane),
        P(HEAD, plane),
        P(HEAD, plane),
        P(plane, HEAD),
    )
    return jax.shard_map(
        local,
        mesh=fine,
        in_specs=placed,
        out_specs=(P(HEAD, plane), P(plane, HEAD)),
        check_vma=False,
    )
```

```python
import jax
import jax.numpy as jnp
from jax import lax
from jax.experimental import pallas as pl
from jax.experimental.pallas import tpu as pltpu
from jax.sharding import Mesh, PartitionSpec as P

HEADS = 64
KV_HEADS = 8
HEAD_DIM = 128
D = 8192
X = ("xh", "xl")
HEAD = ("y", "c")
ALL = ("xh", "z", "y", "c", "xl")
BF = jnp.bfloat16
F4 = jnp.float32


def shift(array, axis, size, step):
    return lax.ppermute(array, axis, [(i, (i + step) % size) for i in range(size)])


def copies_by_a2a(array, axis, size):
    copies = jnp.broadcast_to(array, (size, *array.shape))
    return lax.all_to_all(copies, axis, 0, 0, tiled=True)


def gather4(array, axis, me):
    got = [array] + [shift(array, axis, 4, k) for k in (1, 3, 2)]
    rel = jnp.stack([got[0], got[1], got[3], got[2]])
    return jnp.stack([lax.dynamic_index_in_dim(rel, (me - j) % 4, 0, False) for j in range(4)])


def summed4(pieces, axis, me):
    send = lambda k: lax.dynamic_index_in_dim(pieces, (me + k) % 4, 0, False).astype(BF)
    got = [shift(send(k), axis, 4, k) for k in (1, 3, 2)]
    own = lax.dynamic_index_in_dim(pieces, me, 0, False).astype(F4)
    return own + got[0].astype(F4) + got[1].astype(F4) + got[2].astype(F4)


def swapped(array, axis):
    return lax.ppermute(array, axis, [(0, 1), (1, 0)])


def device_pairs(place):
    pairs = []
    for xh in range(2):
        for z in range(8):
            for y in range(4):
                for c in range(2):
                    for xl in range(2):
                        src = (((xh * 8 + z) * 4 + y) * 2 + c) * 2 + xl
                        nxh, nz, ny, nc, nxl = place(xh, z, y, c, xl)
                        pairs.append((src, (((nxh * 8 + nz) * 4 + ny) * 2 + nc) * 2 + nxl))
    return pairs


def to_features(xh, z, y, c, xl):
    return xh, ((y & 1) << 2) | (c << 1) | (z & 1), (y & 2) | (z >> 2), (z >> 1) & 1, xl


def swap_same(xh, z, y, c, xl):
    return y >> 1, z, (xh << 1) | (y & 1), c, xl


def swap_cross(xh, z, y, c, xl):
    return y >> 1, z, (xh << 1) | (y & 1), c, 1 - xl


VM = pl.BlockSpec(memory_space=pltpu.VMEM)
SM = pl.BlockSpec(memory_space=pltpu.SMEM)
CHUNKS = 2


def attention_body(lengths, q, kn, vn, k_hbm, v_hbm, out, keys, values, mixed, sems):
    row_count, slots = keys.shape[0], keys.shape[1]
    step = row_count // CHUNKS
    copies = []
    for n in range(CHUNKS):
        cut = pl.ds(n * step, step)
        copies.append(pltpu.make_async_copy(k_hbm.at[cut], keys.at[cut], sems.at[0, n]))
        copies.append(pltpu.make_async_copy(v_hbm.at[cut], values.at[cut], sems.at[1, n]))
    for copy in copies:
        copy.start()
    group = HEADS // KV_HEADS
    scale = HEAD_DIM ** (-0.5)
    slot_ids = lax.broadcasted_iota(jnp.int32, (group, slots), 1)
    heads = [q[:, HEAD_DIM * g : HEAD_DIM * (g + 1)].astype(F4) for g in range(group)]
    new_keys = kn[...].astype(F4)
    new_values = vn[...].astype(F4)
    for n in range(CHUNKS):
        rows = range(n * step, n * step + step)
        qs = [jnp.concatenate([h[r : r + 1] for h in heads], axis=0) for r in rows]
        copies[2 * n].wait()
        ws, tots, owns = [], [], []
        for r, qr in zip(rows, qs):
            s = lax.dot_general(
                qr.astype(BF), keys[r], (((1,), (1,)), ((), ())), preferred_element_type=F4
            )
            s = jnp.where(slot_ids < lengths[r], s * scale, -jnp.inf)
            own = jnp.sum(qr * new_keys[r : r + 1], axis=1, keepdims=True) * scale
            top = jnp.maximum(jnp.max(s, axis=1, keepdims=True), own)
            w = jnp.exp(s - top)
            own = jnp.exp(own - top)
            tots.append(jnp.sum(w, axis=1, keepdims=True) + own)
            ws.append(w.astype(BF))
            owns.append(own.astype(BF).astype(F4))
        copies[2 * n + 1].wait()
        for r, w, tot, own in zip(rows, ws, tots, owns):
            mix = jnp.dot(w, values[r], preferred_element_type=F4) + own * new_values[r : r + 1]
            mix = mix / tot
            for g in range(group):
                mixed[r : r + 1, HEAD_DIM * g : HEAD_DIM * (g + 1)] = mix[g : g + 1]
    attn = mixed[...].astype(BF)
    for j in range(out.shape[0]):
        out[j] = attn


def attention(queries, new_keys, new_values, key_cache, value_cache, lengths, copies):
    rows, slots, dim = key_cache.shape
    width = queries.shape[1]
    anywhere = pl.BlockSpec(memory_space=pl.ANY)
    return pl.pallas_call(
        attention_body,
        out_shape=jax.ShapeDtypeStruct((copies, rows, width), BF),
        in_specs=[SM, VM, VM, VM, anywhere, anywhere],
        out_specs=VM,
        scratch_shapes=[
            pltpu.VMEM((rows, slots, dim), BF),
            pltpu.VMEM((rows, slots, dim), BF),
            pltpu.VMEM((rows, width), F4),
            pltpu.SemaphoreType.DMA((2, CHUNKS)),
        ],
        compiler_params=pltpu.CompilerParams(vmem_limit_bytes=60 * 1024 * 1024),
        cost_estimate=pl.CostEstimate(
            flops=4 * rows * width * slots, bytes_accessed=4 * rows * slots * dim, transcendentals=0
        ),
    )(lengths, queries, new_keys, new_values, key_cache, value_cache)


N_CUTS = ((0, 256), (256, 256), (512, 256), (768, 128))


def call(body, outs, ins, scratch=(), flops=0):
    moved = sum(a.size * a.dtype.itemsize for a in ins)
    return pl.pallas_call(
        body,
        out_shape=outs,
        in_specs=[SM] + [VM] * (len(ins) - 1),
        out_specs=jax.tree.map(lambda _: VM, outs),
        scratch_shapes=list(scratch),
        compiler_params=pltpu.CompilerParams(vmem_limit_bytes=40 * 1024 * 1024),
        cost_estimate=pl.CostEstimate(flops=flops, bytes_accessed=moved, transcendentals=0),
    )(*ins)


def sds(shape, dtype):
    return jax.ShapeDtypeStruct(shape, dtype)


def proj_body(at, rows, w0, w1, w2, w3, out):
    for k, w in enumerate((w0, w1, w2, w3)):
        src = lax.rem(at[0] + 4 - k, 4)
        xh, xl = lax.div(src, 2), lax.rem(src, 2)
        part = jnp.dot(rows[...], w[...], preferred_element_type=F4)
        for j in range(4):
            out[xh * 4 + j, xl] = part[24 * j : 24 * j + 24].astype(BF)


def proj(at, rows, weights):
    return call(proj_body, sds((8, 2, 24, 256), BF), [at, rows, *weights], flops=2 * 96 * 1024 * 1024)


def first_body(at, p0, wg, wu, out):
    part = p0[...].astype(F4)
    part = part * part
    out[...] = part[:, :, :128] + part[:, :, 128:256] + part[:, :, 256:384] + part[:, :, 384:]


def up_body(half, at, sq0, p0, p1, p2, p3, gain, wg, wu, out, rows, squares):
    z1 = at[2] if half == 0 else 1 - at[2]
    for k, p in enumerate((p0, p1, p2, p3)):
        src = lax.rem(at[0] + 4 - k, 4)
        xh, xl = lax.div(src, 2), lax.rem(src, 2)
        for z2 in range(2):
            row = pl.multiple_of(xh * 96 + z2 * 48 + xl * 24, 8)
            sq = None
            for z0 in range(2):
                place = z2 * 4 + z1 * 2 + z0
                part = p[place].astype(F4)
                cols = slice(z0 * 512, z0 * 512 + 512)
                rows[pl.ds(row, 24), cols] = part * gain[:, cols]
                if k == 0:
                    one = sq0[place]
                else:
                    part = part * part
                    one = part[:, :128] + part[:, 128:256] + part[:, 256:384] + part[:, 384:]
                sq = one if sq is None else sq + one
            squares[pl.ds(row, 24), :] = sq
    total = jnp.sum(squares[...], axis=1, keepdims=True)
    high = total.astype(BF).astype(F4)
    lanes = lax.broadcasted_iota(jnp.int32, (192, 128), 1)
    tail = jnp.where(lanes == 0, high, jnp.where(lanes == 1, total - high, 0.0))
    left = rows[...].astype(BF)
    for base, w in ((0, wg), (896, wu)):
        for at_col, size in N_CUTS:
            part = jnp.dot(left, w[:, at_col : at_col + size], preferred_element_type=F4)
            part = part.astype(out.dtype).reshape(4, 48, size)
            out[:, :, base + at_col : base + at_col + size] = part
    out[:, :, 1792:] = tail.astype(out.dtype).reshape(4, 48, 128)


def up_half(half, dtype, at, sq0, pieces, gain, wg, wu):
    return call(
        lambda *refs: up_body(half, *refs),
        sds((4, 48, 1920), dtype),
        [at, sq0, *pieces, gain, wg, wu],
        [pltpu.VMEM((192, 1024), F4), pltpu.VMEM((192, 128), F4)],
        flops=2 * 192 * 1024 * 1792,
    )


def pair_body(at, mine, theirs, own, s1, s2, s3):
    y = at[1]
    own[...] = mine[y] + theirs[y].astype(F4)
    for k, ref in ((1, s1), (2, s2), (3, s3)):
        to = lax.rem(y + k, 4)
        ref[...] = (mine[to] + theirs[to].astype(F4)).astype(BF)


def pair_sums(at, mine, theirs):
    outs = [sds((48, 1920), F4)] + [sds((48, 1920), BF)] * 3
    return call(pair_body, outs, [at, mine, theirs])


def hidden_body(at, own, r1, r2, r3, out):
    add = lambda lo, hi: (
        own[:, lo:hi] + r1[:, lo:hi].astype(F4) + r2[:, lo:hi].astype(F4) + r3[:, lo:hi].astype(F4)
    )
    mean_square = jnp.sum(add(1792, 1920), axis=1, keepdims=True) / D
    inv = lax.rsqrt(mean_square + 1e-05)
    gate = add(0, 896) * inv
    up = add(896, 1792) * inv
    out[...] = (gate / (1.0 + jnp.exp(-gate)) * up).astype(BF)


def order_body(at, p0, p1, p2, p3, out):
    for k, p in enumerate((p0, p1, p2, p3)):
        out[lax.rem(at[1] + 4 - k, 4)] = p[...]


def down_body(at, mine, theirs, w, own, s1, s2, s3, acc):
    for rows, z1 in ((mine, at[2]), (theirs, 1 - at[2])):
        left = rows[...].reshape(192, 896)
        for n in range(4):
            part = jnp.dot(left, w[:, 256 * n : 256 * n + 256], preferred_element_type=F4)
            for b in range(4):
                for xl in range(2):
                    r = b * 48 + xl * 24
                    acc[(b // 2) * 2 + xl, (b % 2) * 2 + z1, :, 256 * n : 256 * n + 256] = part[r : r + 24]
    own[...] = acc[at[0]]
    for k, ref in ((1, s1), (2, s2), (3, s3)):
        ref[...] = acc[lax.rem(at[0] + k, 4)].astype(BF)


def down(at, mine, theirs, weight):
    outs = [sds((4, 24, 1024), F4)] + [sds((4, 24, 1024), BF)] * 3
    return call(
        down_body,
        outs,
        [at, mine, theirs, weight],
        [pltpu.VMEM((4, 4, 24, 1024), F4)],
        flops=2 * 384 * 896 * 1024,
    )


def around(array, axis):
    got = {k: shift(array, axis, 4, k) for k in (2, 1, 3)}
    return [got[1], got[2], got[3]]


def sent(one, two, three, axis):
    got = {k: shift(a, axis, 4, k) for k, a in ((2, two), (1, one), (3, three))}
    return [got[1], got[2], got[3]]


def local(
    queries,
    new_keys,
    new_values,
    key_cache,
    value_cache,
    lengths,
    residual,
    norm_gain,
    out_weight,
    gate_weight,
    up_weight,
    down_weight,
):
    x = lax.axis_index("xh") * 2 + lax.axis_index("xl")
    y = lax.axis_index("y")
    c = lax.axis_index("c")
    at = jnp.stack([x, y, c, c]).astype(jnp.int32)
    xl = lax.axis_index("xl")
    gain = lax.dynamic_slice_in_dim(norm_gain, (y * 2 + c) * 1024, 1024, 0).reshape(1, 1024)
    weights = [out_weight, *around(out_weight, X)]

    attn = attention(queries, new_keys, new_values, key_cache, value_cache, lengths, 8)
    rows = lax.all_to_all(attn, "z", 0, 0, tiled=True).reshape(96, 1024)
    res = residual.reshape(2, 2, 12, 256).swapaxes(0, 1)
    res, _ = lax.optimization_barrier((res, attn))
    res_same = lax.dynamic_index_in_dim(res, xl, 0, False).reshape(24, 256)
    res_cross = lax.dynamic_index_in_dim(res, 1 - xl, 0, False).reshape(24, 256)
    res_same = lax.ppermute(res_same, ALL, device_pairs(swap_same))
    res_cross = lax.ppermute(res_cross, ALL, device_pairs(swap_cross))
    first = jnp.where(xl == 0, res_same, res_cross).astype(F4)
    second = jnp.where(xl == 0, res_cross, res_same).astype(F4)
    pieces = lax.all_to_all(proj(at, rows, weights), HEAD, 0, 0, tiled=True)
    state = jnp.sum(pieces.astype(F4), axis=0) + jnp.stack([first, second])
    state = state.astype(BF)

    moved = state.swapaxes(0, 1).reshape(24, 512)
    moved = lax.ppermute(moved, ALL, device_pairs(to_features))
    out_same = lax.dynamic_index_in_dim(state, xl, 0, False)
    out_cross = lax.dynamic_index_in_dim(state, 1 - xl, 0, False)
    out_same = lax.ppermute(out_same, ALL, device_pairs(swap_same))
    out_cross = lax.ppermute(out_cross, ALL, device_pairs(swap_cross))
    hidden_state = jnp.stack([jnp.where(xl == 0, out_same, out_cross), jnp.where(xl == 0, out_cross, out_same)])
    hidden_state = hidden_state.reshape(2, 2, 12, 256).swapaxes(0, 1).reshape(48, 256)

    along_z = copies_by_a2a(moved, "z", 8)
    pieces = [along_z, *around(along_z, X)]
    sq0 = call(first_body, sds((8, 24, 128), F4), [at, along_z, gate_weight, up_weight])
    other = up_half(1, BF, at, sq0, pieces, gain, gate_weight, up_weight)
    theirs = swapped(other, "c")
    mine = up_half(0, F4, at, sq0, pieces, gain, gate_weight, up_weight)
    own, *shares = pair_sums(at, mine, theirs)
    hidden = call(hidden_body, sds((48, 896), BF), [at, own, *sent(*shares, "y")])
    hidden = call(order_body, sds((4, 48, 896), BF), [at, hidden, *around(hidden, "y")])
    own, *shares = down(at, hidden, swapped(hidden, "c"), down_weight)
    part = own
    for got in sent(*shares, X):
        part = part + got.astype(F4)
    part = part.astype(BF).reshape(8, 12, 1024)
    part = lax.all_to_all(part, "z", 0, 0, tiled=True)
    ffn_out = jnp.sum(part.astype(F4), axis=0).astype(BF)
    return (hidden_state, ffn_out)


def solution(mesh):
    fine = Mesh(mesh.devices.reshape(2, 8, 4, 2, 2), ALL)
    plane = ("xh", "z", "xl")
    placed = (
        P(plane, HEAD),
        P(plane, HEAD),
        P(plane, HEAD),
        P(plane, None, HEAD),
        P(plane, None, HEAD),
        P(plane),
        P(HEAD, plane),
        P(),
        P(HEAD, plane),
        P(HEAD, plane),
        P(HEAD, plane),
        P(plane, HEAD),
    )
    return jax.shard_map(
        local,
        mesh=fine,
        in_specs=placed,
        out_specs=(P(HEAD, plane), P(plane, HEAD)),
        check_vma=False,
    )
```

```python
import jax
import jax.numpy as jnp
from jax import lax
from jax.experimental import pallas as pl
from jax.experimental.pallas import tpu as pltpu
from jax.sharding import Mesh, PartitionSpec as P

HEADS = 64
KV_HEADS = 8
HEAD_DIM = 128
D = 8192
X = ("xh", "xl")
HEAD = ("y", "c")
ALL = ("xh", "z", "y", "c", "xl")
BF = jnp.bfloat16
F4 = jnp.float32


def shift(array, axis, size, step):
    return lax.ppermute(array, axis, [(i, (i + step) % size) for i in range(size)])


def copies_by_a2a(array, axis, size):
    copies = jnp.broadcast_to(array, (size, *array.shape))
    return lax.all_to_all(copies, axis, 0, 0, tiled=True)


def gather4(array, axis, me):
    got = [array] + [shift(array, axis, 4, k) for k in (1, 3, 2)]
    rel = jnp.stack([got[0], got[1], got[3], got[2]])
    return jnp.stack([lax.dynamic_index_in_dim(rel, (me - j) % 4, 0, False) for j in range(4)])


def summed4(pieces, axis, me):
    send = lambda k: lax.dynamic_index_in_dim(pieces, (me + k) % 4, 0, False).astype(BF)
    got = [shift(send(k), axis, 4, k) for k in (1, 3, 2)]
    own = lax.dynamic_index_in_dim(pieces, me, 0, False).astype(F4)
    return own + got[0].astype(F4) + got[1].astype(F4) + got[2].astype(F4)


def swapped(array, axis):
    return lax.ppermute(array, axis, [(0, 1), (1, 0)])


def device_pairs(place):
    pairs = []
    for xh in range(2):
        for z in range(8):
            for y in range(4):
                for c in range(2):
                    for xl in range(2):
                        src = (((xh * 8 + z) * 4 + y) * 2 + c) * 2 + xl
                        nxh, nz, ny, nc, nxl = place(xh, z, y, c, xl)
                        pairs.append((src, (((nxh * 8 + nz) * 4 + ny) * 2 + nc) * 2 + nxl))
    return pairs


def to_features(xh, z, y, c, xl):
    return xh, ((y & 1) << 2) | (c << 1) | (z & 1), (y & 2) | (z >> 2), (z >> 1) & 1, xl


def swap_same(xh, z, y, c, xl):
    return y >> 1, z, (xh << 1) | (y & 1), c, xl


def swap_cross(xh, z, y, c, xl):
    return y >> 1, z, (xh << 1) | (y & 1), c, 1 - xl


VM = pl.BlockSpec(memory_space=pltpu.VMEM)
SM = pl.BlockSpec(memory_space=pltpu.SMEM)
CHUNKS = 2


def attention_body(lengths, q, kn, vn, k_hbm, v_hbm, out, keys, values, mixed, sems):
    row_count, slots = keys.shape[0], keys.shape[1]
    step = row_count // CHUNKS
    copies = []
    for n in range(CHUNKS):
        cut = pl.ds(n * step, step)
        copies.append(pltpu.make_async_copy(k_hbm.at[cut], keys.at[cut], sems.at[0, n]))
        copies.append(pltpu.make_async_copy(v_hbm.at[cut], values.at[cut], sems.at[1, n]))
    for copy in copies:
        copy.start()
    group = HEADS // KV_HEADS
    scale = HEAD_DIM ** (-0.5)
    slot_ids = lax.broadcasted_iota(jnp.int32, (group, slots), 1)
    heads = [q[:, HEAD_DIM * g : HEAD_DIM * (g + 1)].astype(F4) for g in range(group)]
    new_keys = kn[...].astype(F4)
    new_values = vn[...].astype(F4)
    for n in range(CHUNKS):
        rows = range(n * step, n * step + step)
        qs = [jnp.concatenate([h[r : r + 1] for h in heads], axis=0) for r in rows]
        copies[2 * n].wait()
        ws, tots, owns = [], [], []
        for r, qr in zip(rows, qs):
            s = lax.dot_general(
                qr.astype(BF), keys[r], (((1,), (1,)), ((), ())), preferred_element_type=F4
            )
            s = jnp.where(slot_ids < lengths[r], s * scale, -jnp.inf)
            own = jnp.sum(qr * new_keys[r : r + 1], axis=1, keepdims=True) * scale
            top = jnp.maximum(jnp.max(s, axis=1, keepdims=True), own)
            w = jnp.exp(s - top)
            own = jnp.exp(own - top)
            tots.append(jnp.sum(w, axis=1, keepdims=True) + own)
            ws.append(w.astype(BF))
            owns.append(own.astype(BF).astype(F4))
        copies[2 * n + 1].wait()
        for r, w, tot, own in zip(rows, ws, tots, owns):
            mix = jnp.dot(w, values[r], preferred_element_type=F4) + own * new_values[r : r + 1]
            mix = mix / tot
            for g in range(group):
                mixed[r : r + 1, HEAD_DIM * g : HEAD_DIM * (g + 1)] = mix[g : g + 1]
    attn = mixed[...].astype(BF)
    for j in range(out.shape[0]):
        out[j] = attn


def attention(queries, new_keys, new_values, key_cache, value_cache, lengths, copies):
    rows, slots, dim = key_cache.shape
    width = queries.shape[1]
    anywhere = pl.BlockSpec(memory_space=pl.ANY)
    return pl.pallas_call(
        attention_body,
        out_shape=jax.ShapeDtypeStruct((copies, rows, width), BF),
        in_specs=[SM, VM, VM, VM, anywhere, anywhere],
        out_specs=VM,
        scratch_shapes=[
            pltpu.VMEM((rows, slots, dim), BF),
            pltpu.VMEM((rows, slots, dim), BF),
            pltpu.VMEM((rows, width), F4),
            pltpu.SemaphoreType.DMA((2, CHUNKS)),
        ],
        compiler_params=pltpu.CompilerParams(vmem_limit_bytes=60 * 1024 * 1024),
        cost_estimate=pl.CostEstimate(
            flops=4 * rows * width * slots, bytes_accessed=4 * rows * slots * dim, transcendentals=0
        ),
    )(lengths, queries, new_keys, new_values, key_cache, value_cache)


N_CUTS = ((0, 256), (256, 256), (512, 256), (768, 128))


def call(body, outs, ins, scratch=(), flops=0):
    moved = sum(a.size * a.dtype.itemsize for a in ins)
    return pl.pallas_call(
        body,
        out_shape=outs,
        in_specs=[SM] + [VM] * (len(ins) - 1),
        out_specs=jax.tree.map(lambda _: VM, outs),
        scratch_shapes=list(scratch),
        compiler_params=pltpu.CompilerParams(vmem_limit_bytes=40 * 1024 * 1024),
        cost_estimate=pl.CostEstimate(flops=flops, bytes_accessed=moved, transcendentals=0),
    )(*ins)


def sds(shape, dtype):
    return jax.ShapeDtypeStruct(shape, dtype)


def proj_body(at, rows, w0, w1, w2, w3, out):
    for k, w in enumerate((w0, w1, w2, w3)):
        src = lax.rem(at[0] + 4 - k, 4)
        xh, xl = lax.div(src, 2), lax.rem(src, 2)
        part = jnp.dot(rows[...], w[...], preferred_element_type=F4)
        for j in range(4):
            out[xh * 4 + j, xl] = part[24 * j : 24 * j + 24].astype(BF)


def proj(at, rows, weights):
    return call(proj_body, sds((8, 2, 24, 256), BF), [at, rows, *weights], flops=2 * 96 * 1024 * 1024)


def first_body(at, p0, wg, wu, out):
    part = p0[...].astype(F4)
    part = part * part
    out[...] = part[:, :, :128] + part[:, :, 128:256] + part[:, :, 256:384] + part[:, :, 384:]


def up_body(half, at, sq0, p0, p1, p2, p3, gain, wg, wu, out, rows, squares):
    z1 = at[2] if half == 0 else 1 - at[2]
    for k, p in enumerate((p0, p1, p2, p3)):
        src = lax.rem(at[0] + 4 - k, 4)
        xh, xl = lax.div(src, 2), lax.rem(src, 2)
        for z2 in range(2):
            row = pl.multiple_of(xh * 96 + z2 * 48 + xl * 24, 8)
            sq = None
            for z0 in range(2):
                place = z2 * 4 + z1 * 2 + z0
                part = p[place].astype(F4)
                cols = slice(z0 * 512, z0 * 512 + 512)
                rows[pl.ds(row, 24), cols] = part * gain[:, cols]
                if k == 0:
                    one = sq0[place]
                else:
                    part = part * part
                    one = part[:, :128] + part[:, 128:256] + part[:, 256:384] + part[:, 384:]
                sq = one if sq is None else sq + one
            squares[pl.ds(row, 24), :] = sq
    total = jnp.sum(squares[...], axis=1, keepdims=True)
    high = total.astype(BF).astype(F4)
    lanes = lax.broadcasted_iota(jnp.int32, (192, 128), 1)
    tail = jnp.where(lanes == 0, high, jnp.where(lanes == 1, total - high, 0.0))
    left = rows[...].astype(BF)
    for base, w in ((0, wg), (896, wu)):
        for at_col, size in N_CUTS:
            part = jnp.dot(left, w[:, at_col : at_col + size], preferred_element_type=F4)
            part = part.astype(out.dtype).reshape(4, 48, size)
            out[:, :, base + at_col : base + at_col + size] = part
    out[:, :, 1792:] = tail.astype(out.dtype).reshape(4, 48, 128)


def up_half(half, dtype, at, sq0, pieces, gain, wg, wu):
    return call(
        lambda *refs: up_body(half, *refs),
        sds((4, 48, 1920), dtype),
        [at, sq0, *pieces, gain, wg, wu],
        [pltpu.VMEM((192, 1024), F4), pltpu.VMEM((192, 128), F4)],
        flops=2 * 192 * 1024 * 1792,
    )


def pair_body(at, mine, theirs, own, s1, s2, s3):
    y = at[1]
    own[...] = mine[y] + theirs[y].astype(F4)
    for k, ref in ((1, s1), (2, s2), (3, s3)):
        to = lax.rem(y + k, 4)
        ref[...] = (mine[to] + theirs[to].astype(F4)).astype(BF)


def pair_sums(at, mine, theirs):
    outs = [sds((48, 1920), F4)] + [sds((48, 1920), BF)] * 3
    return call(pair_body, outs, [at, mine, theirs])


def hidden_body(at, own, r1, r2, r3, out):
    add = lambda lo, hi: (
        own[:, lo:hi] + r1[:, lo:hi].astype(F4) + r2[:, lo:hi].astype(F4) + r3[:, lo:hi].astype(F4)
    )
    mean_square = jnp.sum(add(1792, 1920), axis=1, keepdims=True) / D
    inv = lax.rsqrt(mean_square + 1e-05)
    gate = add(0, 896) * inv
    up = add(896, 1792) * inv
    out[...] = (gate / (1.0 + jnp.exp(-gate)) * up).astype(BF)


def order_body(at, p0, p1, p2, p3, out):
    for k, p in enumerate((p0, p1, p2, p3)):
        out[lax.rem(at[1] + 4 - k, 4)] = p[...]


def down_rows(rows, w, acc):
    left = rows[...].reshape(192, 896)
    for n in range(4):
        part = jnp.dot(left, w[:, 256 * n : 256 * n + 256], preferred_element_type=F4)
        for b in range(4):
            for xl in range(2):
                r = b * 48 + xl * 24
                acc[(b // 2) * 2 + xl, b % 2, :, 256 * n : 256 * n + 256] = part[r : r + 24]


def down_mine_body(at, mine, w, acc):
    down_rows(mine, w, acc)


def down_body(at, ready, theirs, w, own, s1, s2, s3, acc):
    down_rows(theirs, w, acc)
    for k, ref in enumerate((own, s1, s2, s3)):
        to = lax.rem(at[0] + k, 4)
        for z2 in range(2):
            ref[z2 * 2 + at[2]] = ready[to, z2].astype(ref.dtype)
            ref[z2 * 2 + 1 - at[2]] = acc[to, z2].astype(ref.dtype)


def down(at, mine, weight):
    outs = [sds((4, 24, 1024), F4)] + [sds((4, 24, 1024), BF)] * 3
    acc = (4, 2, 24, 1024)
    theirs = swapped(mine, "c")
    flops = 192 * 896 * 1024 * 2
    ready = call(down_mine_body, sds(acc, F4), [at, mine, weight], flops=flops)
    return call(down_body, outs, [at, ready, theirs, weight], [pltpu.VMEM(acc, F4)], flops=flops)


def last_body(at, own, r1, r2, r3, out):
    for j in range(4):
        total = own[j] + r1[j].astype(F4) + r2[j].astype(F4) + r3[j].astype(F4)
        out[2 * j] = total[:12].astype(BF)
        out[2 * j + 1] = total[12:].astype(BF)


def around(array, axis):
    got = {k: shift(array, axis, 4, k) for k in (2, 1, 3)}
    return [got[1], got[2], got[3]]


def sent(one, two, three, axis):
    got = {k: shift(a, axis, 4, k) for k, a in ((2, two), (1, one), (3, three))}
    return [got[1], got[2], got[3]]


def local(
    queries,
    new_keys,
    new_values,
    key_cache,
    value_cache,
    lengths,
    residual,
    norm_gain,
    out_weight,
    gate_weight,
    up_weight,
    down_weight,
):
    x = lax.axis_index("xh") * 2 + lax.axis_index("xl")
    y = lax.axis_index("y")
    c = lax.axis_index("c")
    at = jnp.stack([x, y, c, c]).astype(jnp.int32)
    xl = lax.axis_index("xl")
    gain = lax.dynamic_slice_in_dim(norm_gain, (y * 2 + c) * 1024, 1024, 0).reshape(1, 1024)
    weights = [out_weight, *around(out_weight, X)]

    attn = attention(queries, new_keys, new_values, key_cache, value_cache, lengths, 8)
    rows = lax.all_to_all(attn, "z", 0, 0, tiled=True).reshape(96, 1024)
    res = residual.reshape(2, 2, 12, 256).swapaxes(0, 1)
    res, _ = lax.optimization_barrier((res, attn))
    res_same = lax.dynamic_index_in_dim(res, xl, 0, False).reshape(24, 256)
    res_cross = lax.dynamic_index_in_dim(res, 1 - xl, 0, False).reshape(24, 256)
    res_same = lax.ppermute(res_same, ALL, device_pairs(swap_same))
    res_cross = lax.ppermute(res_cross, ALL, device_pairs(swap_cross))
    first = jnp.where(xl == 0, res_same, res_cross).astype(F4)
    second = jnp.where(xl == 0, res_cross, res_same).astype(F4)
    pieces = lax.all_to_all(proj(at, rows, weights), HEAD, 0, 0, tiled=True)
    state = jnp.sum(pieces.astype(F4), axis=0) + jnp.stack([first, second])
    state = state.astype(BF)

    moved = state.swapaxes(0, 1).reshape(24, 512)
    moved = lax.ppermute(moved, ALL, device_pairs(to_features))
    out_same = lax.dynamic_index_in_dim(state, xl, 0, False)
    out_cross = lax.dynamic_index_in_dim(state, 1 - xl, 0, False)
    out_same = lax.ppermute(out_same, ALL, device_pairs(swap_same))
    out_cross = lax.ppermute(out_cross, ALL, device_pairs(swap_cross))
    hidden_state = jnp.stack([jnp.where(xl == 0, out_same, out_cross), jnp.where(xl == 0, out_cross, out_same)])
    hidden_state = hidden_state.reshape(2, 2, 12, 256).swapaxes(0, 1).reshape(48, 256)

    along_z = copies_by_a2a(moved, "z", 8)
    pieces = [along_z, *around(along_z, X)]
    sq0 = call(first_body, sds((8, 24, 128), F4), [at, along_z, gate_weight, up_weight])
    other = up_half(1, BF, at, sq0, pieces, gain, gate_weight, up_weight)
    theirs = swapped(other, "c")
    mine = up_half(0, F4, at, sq0, pieces, gain, gate_weight, up_weight)
    own, *shares = pair_sums(at, mine, theirs)
    hidden = call(hidden_body, sds((48, 896), BF), [at, own, *sent(*shares, "y")])
    hidden = call(order_body, sds((4, 48, 896), BF), [at, hidden, *around(hidden, "y")])
    own, *shares = down(at, hidden, down_weight)
    part = call(last_body, sds((8, 12, 1024), BF), [at, own, *sent(*shares, X)])
    part = lax.all_to_all(part, "z", 0, 0, tiled=True)
    ffn_out = jnp.sum(part.astype(F4), axis=0).astype(BF)
    return (hidden_state, ffn_out)


def solution(mesh):
    fine = Mesh(mesh.devices.reshape(2, 8, 4, 2, 2), ALL)
    plane = ("xh", "z", "xl")
    placed = (
        P(plane, HEAD),
        P(plane, HEAD),
        P(plane, HEAD),
        P(plane, None, HEAD),
        P(plane, None, HEAD),
        P(plane),
        P(HEAD, plane),
        P(),
        P(HEAD, plane),
        P(HEAD, plane),
        P(HEAD, plane),
        P(plane, HEAD),
    )
    return jax.shard_map(
        local,
        mesh=fine,
        in_specs=placed,
        out_specs=(P(HEAD, plane), P(plane, HEAD)),
        check_vma=False,
    )
```
